256 devices in a mesh: pass: 64 (over z, x_lo, y), blk: 4 (over x_hi, core).
Axes of the slice: x: 4 (x_hi: 2, x_lo: 2; x = x_hi * 2 + x_lo), y: 4, z: 8, core: 2. Of those that a mesh axis runs over, the one named last changes fastest.
Arguments:
- state: float32 [5, 32, 64, 8192], P(None, None, 'blk', 'pass'), as said below
- partner: int32 [64], replicated, may hold values from 0 to 63, as said below
- stencil: int32 [8192], P('pass'), may hold values from 0 to 15
- weight_table: float32 [16], replicated, may hold values from 0 to 1
Outputs:
- next_state: float32 [5, 32, 64, 8192], P(None, None, 'blk', 'pass')
The draws below stay inside these ranges and needn't reach their ends.
Inputs may be any that keep to these rules, and one draw needn't show every extreme that they name: partner[p] = (p + R) mod 64 for one R of 1 to 63 drawn for each step. `state`: every cell's density lies between 0.6 and 1.6 and its pressure between 0.4 and 1.2.
All inputs are finite; a program needn't handle non-finite values.
Results may differ from the reference program's by a relative error of at most 0.0003.
Values sent between devices are 32-bit elements; how exact they have to be, the bound alone decides.
No kernel may reach another device: no remote copies, remote signals or barrier semaphores. Data moves between devices by JAX's collectives and lax.ppermute only.
A program may use at most 64 MiB of HBM per device.

```python
import jax
import jax.numpy as jnp
from jax import lax

CR = 32
CT = 128
NW = 16
PASSAGES = 64
CIRC = 8192
AX = 64


def draw_state(key, part):
    keys = jax.random.split(jax.random.fold_in(key, 11), 5)
    shape = (CR, AX, CIRC)
    rough = [jax.random.uniform(keys[i], shape, jnp.float32, -1.0, 1.0) for i in range(5)]
    density = jnp.exp(0.35 * rough[0])
    axial_velocity = 0.5 + 0.4 * rough[1]
    radial_velocity = 0.2 * rough[2]
    around_velocity = 0.6 * rough[3]
    pressure = 0.72 * jnp.exp(0.38 * rough[4])
    energy = pressure / 0.4 + 0.5 * density * (axial_velocity * axial_velocity + radial_velocity * radial_velocity + around_velocity * around_velocity)
    return jnp.stack([density, density * axial_velocity, density * radial_velocity, density * around_velocity, energy]).astype(jnp.float32)


def draw_partner(key, part):
    rotation = jax.random.randint(jax.random.fold_in(key, 23), (), 1, PASSAGES)
    return ((jnp.arange(PASSAGES, dtype=jnp.int32) + rotation) % PASSAGES).astype(jnp.int32)


def touch_ends(values, own_key, least, largest):
    place = [jax.random.randint(jax.random.fold_in(own_key, axis), (), 0, length) for axis, length in enumerate(values.shape)]
    widest = values.shape.index(max(values.shape))
    next_to = place[:widest] + [(place[widest] + 1) % values.shape[widest]] + place[widest + 1:]
    return values.at[tuple(place)].set(least).at[tuple(next_to)].set(largest)


def setup_inputs(seed: int = 0) -> dict:
    splits = jax.random.split(jax.random.key(seed), 5)
    state = draw_state(jax.random.fold_in(splits[4], 71), 0)
    partner = draw_partner(jax.random.fold_in(splits[4], 71), 0)
    stencil = touch_ends(jax.random.randint(splits[2], (CIRC,), 0, NW), jax.random.fold_in(splits[2], 1), 0, NW - 1).astype(jnp.int32)
    weight_table = jnp.clip(jax.random.uniform(splits[3], (NW,), jnp.float32, 0.0, 1.0), 0.0, 1.0)
    return {"state": state, "partner": partner, "stencil": stencil, "weight_table": weight_table}


GAMMA_MINUS = 0.4
GAMMA_VALUE = 1.4
AXIAL_COEF = 0.4
RADIAL_COEF = 0.3
AROUND_COEF = 0.3

def cell_parts(cells, component):
    density = cells[0]
    velocity = cells[component] / density
    pressure = GAMMA_MINUS * (cells[4] - 0.5 * (cells[1] * cells[1] + cells[2] * cells[2] + cells[3] * cells[3]) / density)
    sound_speed = jnp.sqrt(GAMMA_VALUE * pressure / density)
    flux = cells * velocity[None]
    flux = flux.at[component].add(pressure)
    flux = flux.at[4].add(pressure * velocity)
    return (flux, jnp.abs(velocity) + sound_speed)

def face_flux(left, right, component):
    flux_left, reach_left = cell_parts(left, component)
    flux_right, reach_right = cell_parts(right, component)
    return 0.5 * (flux_left + flux_right) - 0.5 * jnp.maximum(reach_left, reach_right)[None] * (right - left)

def residual_section(slab, ghost_rotor, ghost_stator, half_point):
    core = slab[:, 1:-1]
    rotor_cells = jnp.concatenate([core[:, :, :1], core[:, :, :half_point], ghost_rotor[:, :, None]], axis=2)
    stator_cells = jnp.concatenate([ghost_stator[:, :, None], core[:, :, half_point:], core[:, :, -1:]], axis=2)
    rotor_faces = face_flux(rotor_cells[:, :, :-1], rotor_cells[:, :, 1:], 1)
    stator_faces = face_flux(stator_cells[:, :, :-1], stator_cells[:, :, 1:], 1)
    axial_diff = jnp.concatenate([rotor_faces[:, :, 1:] - rotor_faces[:, :, :-1], stator_faces[:, :, 1:] - stator_faces[:, :, :-1]], axis=2)
    radial_faces = face_flux(slab[:, :-1], slab[:, 1:], 2)
    radial_diff = radial_faces[:, 1:] - radial_faces[:, :-1]
    beside_all = jnp.concatenate([core[..., -1:], core, core[..., :1]], axis=3)
    around_faces = face_flux(beside_all[..., :-1], beside_all[..., 1:], 3)
    around_diff = around_faces[..., 1:] - around_faces[..., :-1]
    return core - AXIAL_COEF * axial_diff - RADIAL_COEF * radial_diff - AROUND_COEF * around_diff

def reference(state, partner, stencil, weight_table):
    half_point = AX // 2
    shift = (partner[0] % PASSAGES).astype(jnp.int32) * CT
    weights = weight_table[stencil]
    stator_plane = state[:, :, half_point]
    rotor_plane = state[:, :, half_point - 1]
    ghost_rotor = weights * jnp.roll(stator_plane, -shift, axis=2) + (1.0 - weights) * jnp.roll(stator_plane, -shift - 1, axis=2)
    ghost_stator = weights * jnp.roll(rotor_plane, shift, axis=2) + (1.0 - weights) * jnp.roll(rotor_plane, shift + 1, axis=2)
    padded = jnp.concatenate([state[:, :1], state, state[:, -1:]], axis=1)
    block_rows = 4

    def one_block(block_index):
        start = (block_index * block_rows).astype(jnp.int32)
        slab = lax.dynamic_slice_in_dim(padded, start, block_rows + 2, axis=1)
        rotor_part = lax.dynamic_slice_in_dim(ghost_rotor, start, block_rows, axis=1)
        stator_part = lax.dynamic_slice_in_dim(ghost_stator, start, block_rows, axis=1)
        return residual_section(slab, rotor_part, stator_part, half_point)
    stacked = lax.map(one_block, jnp.arange(CR // block_rows, dtype=jnp.int32))
    return jnp.moveaxis(stacked, 0, 1).reshape(5, CR, AX, CIRC)
```

```python
import jax
import jax.numpy as jnp
from jax import lax
from jax.experimental import pallas as pl
from jax.experimental.pallas import tpu as pltpu
from jax.sharding import PartitionSpec as P

AXIAL_HALF = 0.2
RADIAL_HALF = 0.15
AROUND_HALF = 0.15
AXES = ("pass", "blk")
BASE = 8


def roll(value, amount, axis):
    amount = amount % value.shape[axis]
    return value if amount == 0 else pltpu.roll(value, amount, axis)


def primitives(q):
    inverse = 1.0 / q[0]
    u = [q[d] * inverse for d in (1, 2, 3)]
    pressure = 0.4 * (q[4] - 0.5 * (q[1] * u[0] + q[2] * u[1] + q[3] * u[2]))
    sound = jnp.sqrt(1.4 * pressure * inverse)
    return u, pressure, sound, q[4] + pressure


def flux(q, prims, direction):
    u, pressure, sound, enthalpy = prims
    speed = u[direction - 1]
    parts = [q[direction]]
    for k in (1, 2, 3):
        part = q[k] * speed
        parts.append(part + pressure if k == direction else part)
    parts.append(enthalpy * speed)
    return parts, jnp.abs(speed) + sound


def faces(flux_left, flux_right, left, right, reach):
    return [
        (fl + fr) - reach * (r - l) for fl, fr, l, r in zip(flux_left, flux_right, left, right)
    ]


def faces_of(left, right, direction):
    flux_left, reach_left = flux(left, primitives(left), direction)
    flux_right, reach_right = flux(right, primitives(right), direction)
    return faces(flux_left, flux_right, left, right, jnp.maximum(reach_left, reach_right))


def pack_kernel(blk_ref, x_ref, bottom_ref, top_ref, axial_ref, inter_ref, edge_ref, around_ref):
    fields, rows, depth, lanes = x_ref.shape
    even = blk_ref[0] % 2 == 0
    lane = lax.broadcasted_iota(jnp.int32, (8, lanes), 1)
    pair = lane // 2
    halves = depth // 8
    packed = [jnp.zeros((8, lanes), jnp.float32) for _ in range(fields)]
    for r in range(rows):
        for h in range(halves):
            k = r * halves + h
            mine = pair == k
            for f in range(fields):
                tile = x_ref[f, r, 8 * h : 8 * h + 8, :]
                packed[f] = jnp.where(mine, roll(tile, 2 * k + 1, 1), packed[f])
    for f in range(fields):
        around_ref[f] = packed[f]
        bottom = x_ref[f, :, 0, :]
        top = x_ref[f, :, depth - 1, :]
        bottom_ref[f] = bottom
        top_ref[f] = top
        axial_ref[f] = jnp.where(even, top, bottom)
        inter_ref[f] = jnp.where(even, bottom, top)
        edge = jnp.zeros((8, lanes), jnp.float32)
        for j in range(rows // 8):
            first = roll(bottom[8 * j : 8 * j + 8], j, 1)
            last = roll(top[8 * j : 8 * j + 8], j + 1, 1)
            edge = jnp.where(lane == j, jnp.where(even, first, last), edge)
        edge_ref[f] = edge


def interior_kernel(x_ref, out_ref):
    fields, rows, depth, lanes = x_ref.shape
    lane = lax.broadcasted_iota(jnp.int32, (depth, lanes), 1)
    level = lax.broadcasted_iota(jnp.int32, (depth, lanes), 0)
    not_last_lane = lane < lanes - 1
    not_last_level = level < depth - 1

    def along(q, prims, direction, axis, size, keep):
        parts, reach = flux(q, prims, direction)
        ahead = [roll(v, size - 1, axis) for v in q]
        parts_ahead = [ahead[direction]] + [roll(v, size - 1, axis) for v in parts[1:]]
        reach = jnp.maximum(reach, roll(reach, size - 1, axis))
        above = faces(parts, parts_ahead, q, ahead, reach)
        above = [jnp.where(keep, v, 0.0) for v in above]
        return [v - roll(v, 1, axis) for v in above]

    def row(r):
        q = [x_ref[f, r] for f in range(fields)]
        prims = primitives(q)
        axial = along(q, prims, 1, 0, depth, not_last_level)
        around = along(q, prims, 3, 1, lanes, not_last_lane)
        partial = [
            v - AXIAL_HALF * a - AROUND_HALF * c for v, a, c in zip(q, axial, around)
        ]
        parts, reach = flux(q, prims, 2)
        return q, parts, reach, partial

    q, parts, reach, partial = row(0)
    partial = [v + (2.0 * RADIAL_HALF) * p for v, p in zip(partial, parts)]

    def step(r, carry):
        q_below, parts_below, reach_below, partial_below = carry
        q, parts, reach, partial = row(r)
        between = faces(parts_below, parts, q_below, q, jnp.maximum(reach_below, reach))
        between = [RADIAL_HALF * v for v in between]
        for f in range(fields):
            out_ref[f, r - 1] = partial_below[f] - between[f]
        return q, parts, reach, [v + b for v, b in zip(partial, between)]

    q, parts, reach, partial = lax.fori_loop(1, rows, step, (q, parts, reach, partial))
    for f in range(fields):
        out_ref[f, rows - 1] = partial[f] - (2.0 * RADIAL_HALF) * parts[f]


def boundary_kernel(
    blk_ref,
    table_ref,
    part_ref,
    bottom_ref,
    top_ref,
    axial_ref,
    plane_ref,
    edge_ref,
    around_ref,
    left_ref,
    right_ref,
    stencil_ref,
    out_ref,
    low_ref,
    high_ref,
):
    fields, rows, depth, lanes = part_ref.shape
    blk = blk_ref[0]
    count = blk_ref[1]
    lane8 = lax.broadcasted_iota(jnp.int32, (8, lanes), 1)
    stencil = jnp.broadcast_to(stencil_ref[...], (8, lanes))
    weights = jnp.zeros((8, lanes), jnp.float32)
    for j in range(table_ref.shape[0]):
        weights = jnp.where(stencil == j, table_ref[j], weights)
    for j in range(rows // 8):
        span = slice(8 * j, 8 * j + 8)
        lower, upper = [], []
        for f in range(fields):
            plane = plane_ref[f, span]
            edge = edge_ref[f]
            ahead = jnp.where(lane8 == lanes - 1, roll(edge, lanes - 1 - j, 1), roll(plane, lanes - 1, 1))
            back = jnp.where(lane8 == 0, roll(edge, lanes - j, 1), roll(plane, 1, 1))
            ghost = weights * plane + (1.0 - weights) * jnp.where(blk % 2 == 0, back, ahead)
            near = axial_ref[f, span]
            lower.append(
                jnp.where(blk == 0, bottom_ref[f, span], jnp.where(blk == count // 2, ghost, near))
            )
            upper.append(
                jnp.where(
                    blk == count - 1, top_ref[f, span], jnp.where(blk == count // 2 - 1, ghost, near)
                )
            )
        below = faces_of(lower, [bottom_ref[f, span] for f in range(fields)], 1)
        above = faces_of([top_ref[f, span] for f in range(fields)], upper, 1)
        for f in range(fields):
            low_ref[f, span] = AXIAL_HALF * below[f]
            high_ref[f, span] = -AXIAL_HALF * above[f]
    even = lane8 % 2 == 0
    own = [around_ref[f] for f in range(fields)]
    lefts = [jnp.where(even, own[f], roll(left_ref[f], 1, 1)) for f in range(fields)]
    rights = [jnp.where(even, roll(right_ref[f], lanes - 1, 1), own[f]) for f in range(fields)]
    sides = faces_of(lefts, rights, 3)
    sides = [jnp.where(even, -AROUND_HALF * v, AROUND_HALF * v) for v in sides]
    ends = (lane8 == 0) | (lane8 == lanes - 1)
    level = lax.broadcasted_iota(jnp.int32, (8, lanes), 0)
    halves = depth // 8
    for r in range(rows):
        for h in range(halves):
            k = r * halves + h
            span = slice(8 * h, 8 * h + 8)
            for f in range(fields):
                tile = part_ref[f, r, span, :]
                tile = tile + jnp.where(ends, roll(sides[f], lanes - 1 - 2 * k, 1), 0.0)
                if h == 0:
                    tile = tile + jnp.where(level == 0, low_ref[f, r : r + 1, :], 0.0)
                if h == halves - 1:
                    tile = tile + jnp.where(level == 7, high_ref[f, r : r + 1, :], 0.0)
                out_ref[f, r, span, :] = tile


def struct(*shape):
    return jax.ShapeDtypeStruct(shape, jnp.float32)


def shards(state, partner, stencil, weight_table):
    blk_count = lax.axis_size("blk")
    cycle_size = lax.axis_size("pass")
    blk_index = lax.axis_index("blk")
    half = blk_count // 2
    fields, rows, depth, lanes = state.shape
    smem = pl.BlockSpec(memory_space=pltpu.SMEM)
    vmem = pl.BlockSpec(memory_space=pltpu.VMEM)
    place = jnp.stack([blk_index, jnp.int32(blk_count)]).astype(jnp.int32)
    plane_shape, tile_shape = struct(fields, rows, lanes), struct(fields, 8, lanes)

    bottom, top, to_axial, to_inter, to_edge, around = pl.pallas_call(
        pack_kernel,
        out_shape=[plane_shape, plane_shape, plane_shape, plane_shape, tile_shape, tile_shape],
        in_specs=[smem, vmem],
        out_specs=[vmem] * 6,
        name="pack",
    )(place, state)

    def at(p, b):
        return (p % cycle_size) * blk_count + b

    axial_pairs = []
    for p in range(cycle_size):
        for b in range(0, blk_count, 2):
            axial_pairs += [(at(p, b), at(p, b + 1)), (at(p, b + 1), at(p, b))]

    def near_pairs(s):
        pairs = []
        for p in range(cycle_size):
            pairs += [(at(p + s, half), at(p, half)), (at(p - s, half - 1), at(p, half - 1))]
        return pairs

    def far_pairs(s):
        pairs = []
        for p in range(cycle_size):
            pairs += [(at(p + s, half), at(p, half - 1)), (at(p - s, half - 1), at(p, half))]
        return pairs

    up = [(i, (i + 1) % cycle_size) for i in range(cycle_size)]
    down = [(j, i) for i, j in up]
    from_left = lax.ppermute(around, "pass", up)
    from_right = lax.ppermute(around, "pass", down)
    from_axial = lax.ppermute(to_axial, AXES, axial_pairs)

    rotation = partner[0] % cycle_size

    def near(s, plane, edge):
        moved = plane if s == 0 else lax.ppermute(plane, AXES, near_pairs(s))
        return moved, lax.ppermute(edge, AXES, near_pairs(s + 1))

    def far(s, plane, edge, cells):
        moved = lax.ppermute(plane, AXES, far_pairs(s)), lax.ppermute(edge, AXES, far_pairs(s))
        part = pl.pallas_call(
            interior_kernel,
            out_shape=struct(*cells.shape),
            in_specs=[vmem],
            out_specs=vmem,
            name="interior",
        )(cells)
        return (*moved, part)

    plane, edge = lax.switch(
        rotation % BASE,
        [lambda a, b, s=s: near(s, a, b) for s in range(BASE)],
        to_inter,
        to_edge,
    )
    plane, edge, part = lax.switch(
        rotation // BASE,
        [lambda a, b, c, s=s: far(s * BASE, a, b, c) for s in range(cycle_size // BASE)],
        plane,
        edge,
        state,
    )
    return pl.pallas_call(
        boundary_kernel,
        out_shape=struct(*state.shape),
        in_specs=[smem, smem] + [vmem] * 10,
        out_specs=vmem,
        scratch_shapes=[pltpu.VMEM((fields, rows, lanes), jnp.float32)] * 2,
        input_output_aliases={2: 0},
        name="boundary",
    )(
        place,
        weight_table,
        part,
        bottom,
        top,
        from_axial,
        plane,
        edge,
        around,
        from_left,
        from_right,
        stencil[None],
    )


def solution(mesh):
    placed = (P(None, None, "blk", "pass"), P(), P("pass"), P())
    return jax.shard_map(
        shards, mesh=mesh, in_specs=placed, out_specs=P(None, None, "blk", "pass"), check_vma=False
    )
```

```python
import functools

import jax
import jax.numpy as jnp
from jax import lax
from jax.experimental import pallas as pl
from jax.experimental.pallas import tpu as pltpu
from jax.sharding import PartitionSpec as P

AXIAL_HALF = 0.2
RADIAL_HALF = 0.15
AROUND_HALF = 0.15
AXES = ("pass", "blk")
VMEM_LIMIT = 16 << 20
CHUNK = 4


def roll(value, amount, axis):
    amount = amount % value.shape[axis]
    return value if amount == 0 else pltpu.roll(value, amount, axis)


def primitives(q):
    inverse = 1.0 / q[0]
    u = [q[d] * inverse for d in (1, 2, 3)]
    pressure = 0.4 * (q[4] - 0.5 * (q[1] * u[0] + q[2] * u[1] + q[3] * u[2]))
    sound = jnp.sqrt(1.4 * pressure * inverse)
    return u, pressure, sound, q[4] + pressure


def flux(q, prims, direction):
    u, pressure, sound, enthalpy = prims
    speed = u[direction - 1]
    parts = [q[direction]]
    for k in (1, 2, 3):
        part = q[k] * speed
        parts.append(part + pressure if k == direction else part)
    parts.append(enthalpy * speed)
    return parts, jnp.abs(speed) + sound


def faces(flux_left, flux_right, left, right, reach):
    return [
        (fl + fr) - reach * (r - l) for fl, fr, l, r in zip(flux_left, flux_right, left, right)
    ]


def faces_of(left, right, direction):
    flux_left, reach_left = flux(left, primitives(left), direction)
    flux_right, reach_right = flux(right, primitives(right), direction)
    return faces(flux_left, flux_right, left, right, jnp.maximum(reach_left, reach_right))


def pack_kernel(
    blk, x_ref, send_ref, own_ref, bottom_ref, top_ref, axial_ref, cells_ref, arrived
):
    fields, rows, depth, lanes = x_ref.shape
    copies = [
        pltpu.make_async_copy(x_ref.at[f], cells_ref.at[f], arrived.at[f]) for f in range(fields)
    ]
    for copy in copies:
        copy.start()
    even = blk() % 2 == 0
    lane = lax.broadcasted_iota(jnp.int32, (8, lanes), 1)
    pair = lane // 2
    halves = depth // 8
    for f in range(fields):
        copies[f].wait()
        packed = [jnp.zeros((8, lanes), jnp.float32) for _ in range(4)]
        for r in range(rows):
            for h in range(halves):
                k = r * halves + h
                tile = cells_ref[f, r, 8 * h : 8 * h + 8, :]
                packed[k % 4] = jnp.where(pair == k, roll(tile, 2 * k + 1, 1), packed[k % 4])
        send_ref[f, rows + 8 : rows + 16] = (packed[0] + packed[1]) + (packed[2] + packed[3])
        bottom = cells_ref[f, :, 0, :]
        top = cells_ref[f, :, depth - 1, :]
        bottom_ref[f] = bottom
        top_ref[f] = top
        axial_ref[f] = jnp.where(even, top, bottom)
        plane = jnp.where(even, bottom, top)
        edge = jnp.zeros((8, lanes), jnp.float32)
        for j in range(rows // 8):
            first = roll(bottom[8 * j : 8 * j + 8], j, 1)
            last = roll(top[8 * j : 8 * j + 8], j + 1, 1)
            edge = jnp.where(lane == j, jnp.where(even, first, last), edge)
        for ref in (send_ref, own_ref):
            ref[f, :rows] = plane
            ref[f, rows : rows + 8] = edge


def interior_kernel(chunk, x_ref, out_ref):
    fields, rows, depth, lanes = x_ref.shape
    lane = lax.broadcasted_iota(jnp.int32, (depth, lanes), 1)
    level = lax.broadcasted_iota(jnp.int32, (depth, lanes), 0)
    not_last_lane = lane < lanes - 1
    not_last_level = level < depth - 1

    def along(q, prims, direction, axis, size, keep):
        parts, reach = flux(q, prims, direction)
        ahead = [roll(v, size - 1, axis) for v in q]
        parts_ahead = [ahead[direction]] + [roll(v, size - 1, axis) for v in parts[1:]]
        reach = jnp.maximum(reach, roll(reach, size - 1, axis))
        above = faces(parts, parts_ahead, q, ahead, reach)
        above = [jnp.where(keep, v, 0.0) for v in above]
        return [v - roll(v, 1, axis) for v in above]

    def row(r):
        q = [x_ref[f, r] for f in range(fields)]
        prims = primitives(q)
        axial = along(q, prims, 1, 0, depth, not_last_level)
        around = along(q, prims, 3, 1, lanes, not_last_lane)
        partial = [
            v - AXIAL_HALF * a - AROUND_HALF * c for v, a, c in zip(q, axial, around)
        ]
        parts, reach = flux(q, prims, 2)
        return q, parts, reach, partial

    def step(i, carry):
        q_below, parts_below, reach_below, partial_below = carry
        for j in range(chunk):
            r = i * chunk + j
            q, parts, reach, partial = row(r)
            between = faces(parts_below, parts, q_below, q, jnp.maximum(reach_below, reach))
            between = [RADIAL_HALF * v for v in between]
            for f in range(fields):
                out_ref[f, jnp.maximum(r - 1, 0)] = partial_below[f] - between[f]
            partial_below = [v + b for v, b in zip(partial, between)]
            q_below, parts_below, reach_below = q, parts, reach
        return q_below, parts_below, reach_below, partial_below

    q = [x_ref[f, 0] for f in range(fields)]
    parts, reach = flux(q, primitives(q), 2)
    q, parts, reach, partial = lax.fori_loop(0, rows // chunk, step, (q, parts, reach, q))
    for f in range(fields):
        out_ref[f, rows - 1] = partial[f] - (2.0 * RADIAL_HALF) * parts[f]


def boundary_kernel(
    blk,
    count,
    table_ref,
    part_ref,
    bottom_ref,
    top_ref,
    axial_ref,
    ghost_ref,
    own_ref,
    left_ref,
    right_ref,
    stencil_ref,
    out_ref,
    low_ref,
    high_ref,
    cells_ref,
    sent,
):
    fields, rows, depth, lanes = part_ref.shape
    halves = depth // 8
    lane8 = lax.broadcasted_iota(jnp.int32, (8, lanes), 1)
    level = lax.broadcasted_iota(jnp.int32, (8, lanes), 0)
    packed = slice(rows + 8, rows + 16)
    here = blk()
    stencil = jnp.broadcast_to(stencil_ref[...], (8, lanes))
    weights = jnp.zeros((8, lanes), jnp.float32)
    for j in range(table_ref.shape[0]):
        weights = jnp.where(stencil == j, table_ref[j], weights)
    for j in range(rows // 8):
        span = slice(8 * j, 8 * j + 8)
        lower, upper = [], []
        for f in range(fields):
            plane = ghost_ref[f, span]
            edge = ghost_ref[f, rows : rows + 8]
            ahead = jnp.where(
                lane8 == lanes - 1, roll(edge, lanes - 1 - j, 1), roll(plane, lanes - 1, 1)
            )
            back = jnp.where(lane8 == 0, roll(edge, lanes - j, 1), roll(plane, 1, 1))
            beside = jnp.where(here % 2 == 0, back, ahead)
            ghost = weights * plane + (1.0 - weights) * beside
            near = axial_ref[f, span]
            below = jnp.where(here == count // 2, ghost, near)
            above = jnp.where(here == count // 2 - 1, ghost, near)
            lower.append(jnp.where(here == 0, bottom_ref[f, span], below))
            upper.append(jnp.where(here == count - 1, top_ref[f, span], above))
        below = faces_of(lower, [bottom_ref[f, span] for f in range(fields)], 1)
        above = faces_of([top_ref[f, span] for f in range(fields)], upper, 1)
        for f in range(fields):
            low_ref[f, span] = AXIAL_HALF * below[f]
            high_ref[f, span] = -AXIAL_HALF * above[f]
    even = lane8 % 2 == 0
    own = [own_ref[f, packed] for f in range(fields)]
    lefts = [jnp.where(even, own[f], roll(left_ref[f, packed], 1, 1)) for f in range(fields)]
    rights = [
        jnp.where(even, roll(right_ref[f, packed], lanes - 1, 1), own[f]) for f in range(fields)
    ]
    sides = faces_of(lefts, rights, 3)
    sides = [jnp.where(even, -AROUND_HALF * v, AROUND_HALF * v) for v in sides]
    ends = (lane8 == 0) | (lane8 == lanes - 1)
    copies = [
        pltpu.make_async_copy(cells_ref.at[f], out_ref.at[f], sent.at[f]) for f in range(fields)
    ]
    for f in range(fields):
        for r in range(rows):
            for h in range(halves):
                k = r * halves + h
                span = slice(8 * h, 8 * h + 8)
                tile = part_ref[f, r, span, :]
                tile = tile + jnp.where(ends, roll(sides[f], lanes - 1 - 2 * k, 1), 0.0)
                if h == 0:
                    tile = tile + jnp.where(level == 0, low_ref[f, r : r + 1, :], 0.0)
                if h == halves - 1:
                    tile = tile + jnp.where(level == 7, high_ref[f, r : r + 1, :], 0.0)
                cells_ref[f, r, span, :] = tile
        copies[f].start()
    for copy in copies:
        copy.wait()


def struct(*shape):
    return jax.ShapeDtypeStruct(shape, jnp.float32)


def shards(state, partner, stencil, weight_table):
    blk_count = lax.axis_size("blk")
    cycle_size = lax.axis_size("pass")
    blk_index = lax.axis_index("blk")
    half = blk_count // 2
    fields, rows, depth, lanes = state.shape
    smem = pl.BlockSpec(memory_space=pltpu.SMEM)
    vmem = pl.BlockSpec(memory_space=pltpu.VMEM)
    anywhere = pl.BlockSpec(memory_space=pl.ANY)
    params = pltpu.CompilerParams(vmem_limit_bytes=VMEM_LIMIT)
    blk = functools.partial(lax.axis_index, "blk")

    send, own, bottom, top, to_axial = pl.pallas_call(
        functools.partial(pack_kernel, blk),
        out_shape=[struct(fields, n, lanes) for n in (rows + 16, rows + 8, rows, rows, rows)],
        in_specs=[anywhere],
        out_specs=[vmem] * 5,
        scratch_shapes=[pltpu.VMEM(state.shape, jnp.float32), pltpu.SemaphoreType.DMA((fields,))],
        compiler_params=params,
        name="pack",
    )(state)

    def at(p, b):
        return (p % cycle_size) * blk_count + b

    axial_pairs = []
    for p in range(cycle_size):
        for b in range(0, blk_count, 2):
            axial_pairs += [(at(p, b), at(p, b + 1)), (at(p, b + 1), at(p, b))]

    def far_pairs(s):
        pairs = []
        for p in range(cycle_size):
            pairs += [(at(p + s, half), at(p, half - 1)), (at(p - s, half - 1), at(p, half))]
        return pairs

    up = [(i, (i + 1) % cycle_size) for i in range(cycle_size)]
    down = [(j, i) for i, j in up]
    from_left = lax.ppermute(send, "pass", up)
    from_right = lax.ppermute(send, "pass", down)
    from_axial = lax.ppermute(to_axial, AXES, axial_pairs)

    rotation = partner[0] % cycle_size
    odd = rotation % 2 == 1
    even = blk_index % 2 == 0
    ahead, back = (v[:, : rows + 8] for v in (from_right, from_left))
    outer, inner = jnp.where(even, ahead, back), jnp.where(even, back, ahead)
    is_edge = lax.broadcasted_iota(jnp.int32, own.shape, 1) >= rows
    payload = jnp.where(
        odd, jnp.where(is_edge, own, inner), jnp.where(is_edge, outer, own)
    )

    def far(s, values, cells):
        moved = lax.ppermute(values, AXES, far_pairs(s))
        part = pl.pallas_call(
            functools.partial(interior_kernel, CHUNK),
            out_shape=struct(*cells.shape),
            in_specs=[vmem],
            out_specs=vmem,
            compiler_params=params,
            name="interior",
        )(cells)
        return moved, part

    ghost, part = lax.switch(
        (rotation + 1) // 2 % (cycle_size // 2),
        [lambda a, c, s=s: far(2 * s, a, c) for s in range(cycle_size // 2)],
        payload,
        state,
    )
    return pl.pallas_call(
        functools.partial(boundary_kernel, blk, blk_count),
        out_shape=struct(*state.shape),
        in_specs=[smem] + [vmem] * 9,
        out_specs=anywhere,
        scratch_shapes=[pltpu.VMEM((fields, rows, lanes), jnp.float32)] * 2
        + [pltpu.VMEM(state.shape, jnp.float32), pltpu.SemaphoreType.DMA((fields,))],
        compiler_params=params,
        name="boundary",
    )(weight_table, part, bottom, top, from_axial, ghost, send, from_left, from_right, stencil[None])


def solution(mesh):
    placed = (P(None, None, "blk", "pass"), P(), P("pass"), P())
    return jax.shard_map(
        shards, mesh=mesh, in_specs=placed, out_specs=P(None, None, "blk", "pass"), check_vma=False
    )
```

```python
import functools

import jax
import jax.numpy as jnp
from jax import lax
from jax.experimental import pallas as pl
from jax.experimental.pallas import tpu as pltpu
from jax.sharding import PartitionSpec as P

AXIAL_HALF = 0.2
RADIAL_HALF = 0.15
AROUND_HALF = 0.15
AXES = ("pass", "blk")
VMEM_LIMIT = 16 << 20
CHUNK = 4


def roll(value, amount, axis):
    amount = amount % value.shape[axis]
    return value if amount == 0 else pltpu.roll(value, amount, axis)


def primitives(q):
    inverse = 1.0 / q[0]
    u = [q[d] * inverse for d in (1, 2, 3)]
    pressure = 0.4 * (q[4] - 0.5 * (q[1] * u[0] + q[2] * u[1] + q[3] * u[2]))
    sound = jnp.sqrt(1.4 * pressure * inverse)
    return u, pressure, sound, q[4] + pressure


def flux(q, prims, direction):
    u, pressure, sound, enthalpy = prims
    speed = u[direction - 1]
    parts = [q[direction]]
    for k in (1, 2, 3):
        part = q[k] * speed
        parts.append(part + pressure if k == direction else part)
    parts.append(enthalpy * speed)
    return parts, jnp.abs(speed) + sound


def faces(flux_left, flux_right, left, right, reach):
    return [
        (fl + fr) - reach * (r - l) for fl, fr, l, r in zip(flux_left, flux_right, left, right)
    ]


def faces_of(left, right, direction):
    flux_left, reach_left = flux(left, primitives(left), direction)
    flux_right, reach_right = flux(right, primitives(right), direction)
    return faces(flux_left, flux_right, left, right, jnp.maximum(reach_left, reach_right))


def pack_kernel(
    blk, x_ref, around_ref, inter_ref, bottom_ref, top_ref, axial_ref, cells_ref, arrived
):
    fields, rows, depth, lanes = x_ref.shape
    copies = [
        pltpu.make_async_copy(x_ref.at[f], cells_ref.at[f], arrived.at[f]) for f in range(fields)
    ]
    for copy in copies:
        copy.start()
    even = blk() % 2 == 0
    lane = lax.broadcasted_iota(jnp.int32, (8, lanes), 1)
    pair = lane // 2
    halves = depth // 8
    for f in range(fields):
        copies[f].wait()
        packed = [jnp.zeros((8, lanes), jnp.float32) for _ in range(4)]
        for r in range(rows):
            for h in range(halves):
                k = r * halves + h
                tile = cells_ref[f, r, 8 * h : 8 * h + 8, :]
                packed[k % 4] = jnp.where(pair == k, roll(tile, 2 * k + 1, 1), packed[k % 4])
        around_ref[f] = (packed[0] + packed[1]) + (packed[2] + packed[3])
        bottom = cells_ref[f, :, 0, :]
        top = cells_ref[f, :, depth - 1, :]
        bottom_ref[f] = bottom
        top_ref[f] = top
        axial_ref[f] = jnp.where(even, top, bottom)
        inter_ref[f] = jnp.where(even, bottom, top)


def interior_kernel(chunk, x_ref, out_ref):
    fields, rows, depth, lanes = x_ref.shape
    lane = lax.broadcasted_iota(jnp.int32, (depth, lanes), 1)
    level = lax.broadcasted_iota(jnp.int32, (depth, lanes), 0)
    not_last_lane = lane < lanes - 1
    not_last_level = level < depth - 1

    def along(q, prims, direction, axis, size, keep):
        parts, reach = flux(q, prims, direction)
        ahead = [roll(v, size - 1, axis) for v in q]
        parts_ahead = [ahead[direction]] + [roll(v, size - 1, axis) for v in parts[1:]]
        reach = jnp.maximum(reach, roll(reach, size - 1, axis))
        above = faces(parts, parts_ahead, q, ahead, reach)
        above = [jnp.where(keep, v, 0.0) for v in above]
        return [v - roll(v, 1, axis) for v in above]

    def row(r):
        q = [x_ref[f, r] for f in range(fields)]
        prims = primitives(q)
        axial = along(q, prims, 1, 0, depth, not_last_level)
        around = along(q, prims, 3, 1, lanes, not_last_lane)
        partial = [
            v - AXIAL_HALF * a - AROUND_HALF * c for v, a, c in zip(q, axial, around)
        ]
        parts, reach = flux(q, prims, 2)
        return q, parts, reach, partial

    def step(i, carry):
        q_below, parts_below, reach_below, partial_below = carry
        for j in range(chunk):
            r = i * chunk + j
            q, parts, reach, partial = row(r)
            between = faces(parts_below, parts, q_below, q, jnp.maximum(reach_below, reach))
            between = [RADIAL_HALF * v for v in between]
            for f in range(fields):
                out_ref[f, jnp.maximum(r - 1, 0)] = partial_below[f] - between[f]
            partial_below = [v + b for v, b in zip(partial, between)]
            q_below, parts_below, reach_below = q, parts, reach
        return q_below, parts_below, reach_below, partial_below

    q = [x_ref[f, 0] for f in range(fields)]
    parts, reach = flux(q, primitives(q), 2)
    q, parts, reach, partial = lax.fori_loop(0, rows // chunk, step, (q, parts, reach, q))
    for f in range(fields):
        out_ref[f, rows - 1] = partial[f] - (2.0 * RADIAL_HALF) * parts[f]


def boundary_kernel(
    blk,
    count,
    table_ref,
    part_ref,
    bottom_ref,
    top_ref,
    axial_ref,
    ghost_ref,
    own_ref,
    left_ref,
    right_ref,
    stencil_ref,
    out_ref,
    low_ref,
    high_ref,
    cells_ref,
    sent,
):
    fields, rows, depth, lanes = part_ref.shape
    halves = depth // 8
    lane8 = lax.broadcasted_iota(jnp.int32, (8, lanes), 1)
    level = lax.broadcasted_iota(jnp.int32, (8, lanes), 0)
    here = blk()
    is_even = here % 2 == 0
    first_lane = jnp.where(is_even, 2 * (halves - 1), 1)
    stencil = jnp.broadcast_to(stencil_ref[...], (8, lanes))
    weights = jnp.zeros((8, lanes), jnp.float32)
    for j in range(table_ref.shape[0]):
        weights = jnp.where(stencil == j, table_ref[j], weights)
    for j in range(rows // 8):
        span = slice(8 * j, 8 * j + 8)
        chosen = lane8 == 2 * halves * (8 * j + level) + first_lane
        end_lane = lane8 == jnp.where(is_even, 0, lanes - 1)
        lower, upper = [], []
        for f in range(fields):
            plane = ghost_ref[f, span]
            packed_row = jnp.where(
                is_even, ghost_ref[f, rows + 7 : rows + 8], ghost_ref[f, rows : rows + 1]
            )
            edge = jnp.sum(jnp.where(chosen, packed_row, 0.0), axis=1, keepdims=True)
            moved = jnp.where(is_even, roll(plane, 1, 1), roll(plane, lanes - 1, 1))
            beside = jnp.where(end_lane, edge, moved)
            ghost = weights * plane + (1.0 - weights) * beside
            near = axial_ref[f, span]
            below = jnp.where(here == count // 2, ghost, near)
            above = jnp.where(here == count // 2 - 1, ghost, near)
            lower.append(jnp.where(here == 0, bottom_ref[f, span], below))
            upper.append(jnp.where(here == count - 1, top_ref[f, span], above))
        below = faces_of(lower, [bottom_ref[f, span] for f in range(fields)], 1)
        above = faces_of([top_ref[f, span] for f in range(fields)], upper, 1)
        for f in range(fields):
            low_ref[f, span] = AXIAL_HALF * below[f]
            high_ref[f, span] = -AXIAL_HALF * above[f]
    even = lane8 % 2 == 0
    own = [own_ref[f] for f in range(fields)]
    lefts = [jnp.where(even, own[f], roll(left_ref[f], 1, 1)) for f in range(fields)]
    rights = [
        jnp.where(even, roll(right_ref[f], lanes - 1, 1), own[f]) for f in range(fields)
    ]
    sides = faces_of(lefts, rights, 3)
    sides = [jnp.where(even, -AROUND_HALF * v, AROUND_HALF * v) for v in sides]
    ends = (lane8 == 0) | (lane8 == lanes - 1)
    copies = [
        pltpu.make_async_copy(cells_ref.at[f], out_ref.at[f], sent.at[f]) for f in range(fields)
    ]
    for f in range(fields):
        for r in range(rows):
            for h in range(halves):
                k = r * halves + h
                span = slice(8 * h, 8 * h + 8)
                tile = part_ref[f, r, span, :]
                tile = tile + jnp.where(ends, roll(sides[f], lanes - 1 - 2 * k, 1), 0.0)
                if h == 0:
                    tile = tile + jnp.where(level == 0, low_ref[f, r : r + 1, :], 0.0)
                if h == halves - 1:
                    tile = tile + jnp.where(level == 7, high_ref[f, r : r + 1, :], 0.0)
                cells_ref[f, r, span, :] = tile
        copies[f].start()
    for copy in copies:
        copy.wait()


def struct(*shape):
    return jax.ShapeDtypeStruct(shape, jnp.float32)


def shards(state, partner, stencil, weight_table):
    blk_count = lax.axis_size("blk")
    cycle_size = lax.axis_size("pass")
    blk_index = lax.axis_index("blk")
    half = blk_count // 2
    fields, rows, depth, lanes = state.shape
    smem = pl.BlockSpec(memory_space=pltpu.SMEM)
    vmem = pl.BlockSpec(memory_space=pltpu.VMEM)
    anywhere = pl.BlockSpec(memory_space=pl.ANY)
    params = pltpu.CompilerParams(vmem_limit_bytes=VMEM_LIMIT)
    blk = functools.partial(lax.axis_index, "blk")

    around, inter, bottom, top, to_axial = pl.pallas_call(
        functools.partial(pack_kernel, blk),
        out_shape=[struct(fields, n, lanes) for n in (8, rows, rows, rows, rows)],
        in_specs=[anywhere],
        out_specs=[vmem] * 5,
        scratch_shapes=[pltpu.VMEM(state.shape, jnp.float32), pltpu.SemaphoreType.DMA((fields,))],
        compiler_params=params,
        name="pack",
    )(state)

    def at(p, b):
        return (p % cycle_size) * blk_count + b

    axial_pairs = []
    for p in range(cycle_size):
        for b in range(0, blk_count, 2):
            axial_pairs += [(at(p, b), at(p, b + 1)), (at(p, b + 1), at(p, b))]

    def far_pairs(s):
        pairs = []
        for p in range(cycle_size):
            pairs += [(at(p + s, half), at(p, half - 1)), (at(p - s, half - 1), at(p, half))]
        return pairs

    up = [(i, (i + 1) % cycle_size) for i in range(cycle_size)]
    down = [(j, i) for i, j in up]
    plane_pairs = []
    for p in range(cycle_size):
        plane_pairs += [(at(p - 1, half), at(p, half)), (at(p + 1, half - 1), at(p, half - 1))]
    from_beside = lax.ppermute(inter, AXES, plane_pairs)
    from_left = lax.ppermute(around, "pass", up)
    from_right = lax.ppermute(around, "pass", down)
    from_axial = lax.ppermute(to_axial, AXES, axial_pairs)

    rotation = partner[0] % cycle_size
    odd = rotation % 2 == 1
    even = blk_index % 2 == 0
    outer = jnp.where(even, from_right, from_left)
    payload = jnp.concatenate(
        [jnp.where(odd, from_beside, inter), jnp.where(odd, around, outer)], axis=1
    )

    def far(s, values, cells):
        moved = lax.ppermute(values, AXES, far_pairs(s))
        part = pl.pallas_call(
            functools.partial(interior_kernel, CHUNK),
            out_shape=struct(*cells.shape),
            in_specs=[vmem],
            out_specs=vmem,
            compiler_params=params,
            name="interior",
        )(cells)
        return moved, part

    ghost, part = lax.switch(
        (rotation + 1) // 2 % (cycle_size // 2),
        [lambda a, c, s=s: far(2 * s, a, c) for s in range(cycle_size // 2)],
        payload,
        state,
    )
    return pl.pallas_call(
        functools.partial(boundary_kernel, blk, blk_count),
        out_shape=struct(*state.shape),
        in_specs=[smem] + [vmem] * 9,
        out_specs=anywhere,
        scratch_shapes=[pltpu.VMEM((fields, rows, lanes), jnp.float32)] * 2
        + [pltpu.VMEM(state.shape, jnp.float32), pltpu.SemaphoreType.DMA((fields,))],
        compiler_params=params,
        name="boundary",
    )(weight_table, part, bottom, top, from_axial, ghost, around, from_left, from_right, stencil[None])


def solution(mesh):
    placed = (P(None, None, "blk", "pass"), P(), P("pass"), P())
    return jax.shard_map(
        shards, mesh=mesh, in_specs=placed, out_specs=P(None, None, "blk", "pass"), check_vma=False
    )
```

```python
import functools

import jax
import jax.numpy as jnp
from jax import lax
from jax.experimental import pallas as pl
from jax.experimental.pallas import tpu as pltpu
from jax.sharding import PartitionSpec as P

AXIAL_HALF = 0.2
RADIAL_HALF = 0.15
AROUND_HALF = 0.15
AXES = ("pass", "blk")
VMEM_LIMIT = 16 << 20
CHUNK = 4


def roll(value, amount, axis):
    amount = amount % value.shape[axis]
    return value if amount == 0 else pltpu.roll(value, amount, axis)


def primitives(q):
    inverse = 1.0 / q[0]
    u = [q[d] * inverse for d in (1, 2, 3)]
    pressure = 0.4 * (q[4] - 0.5 * (q[1] * u[0] + q[2] * u[1] + q[3] * u[2]))
    sound = jnp.sqrt(1.4 * pressure * inverse)
    return u, pressure, sound, q[4] + pressure


def flux(q, prims, direction):
    u, pressure, sound, enthalpy = prims
    speed = u[direction - 1]
    parts = [q[direction]]
    for k in (1, 2, 3):
        part = q[k] * speed
        parts.append(part + pressure if k == direction else part)
    parts.append(enthalpy * speed)
    return parts, jnp.abs(speed) + sound


def faces(flux_left, flux_right, left, right, reach):
    return [
        (fl + fr) - reach * (r - l) for fl, fr, l, r in zip(flux_left, flux_right, left, right)
    ]


def faces_of(left, right, direction):
    flux_left, reach_left = flux(left, primitives(left), direction)
    flux_right, reach_right = flux(right, primitives(right), direction)
    return faces(flux_left, flux_right, left, right, jnp.maximum(reach_left, reach_right))


def pack_kernel(
    blk, x_ref, send_ref, around_ref, bottom_ref, top_ref, axial_ref, cells_ref, arrived
):
    fields, rows, depth, lanes = x_ref.shape
    copies = [
        pltpu.make_async_copy(x_ref.at[f], cells_ref.at[f], arrived.at[f]) for f in range(fields)
    ]
    for copy in copies:
        copy.start()
    even = blk() % 2 == 0
    lane = lax.broadcasted_iota(jnp.int32, (8, lanes), 1)
    pair = lane // 2
    halves = depth // 8
    for f in range(fields):
        copies[f].wait()
        packed = [jnp.zeros((8, lanes), jnp.float32) for _ in range(4)]
        for r in range(rows):
            for h in range(halves):
                k = r * halves + h
                tile = cells_ref[f, r, 8 * h : 8 * h + 8, :]
                packed[k % 4] = jnp.where(pair == k, roll(tile, 2 * k + 1, 1), packed[k % 4])
        around = (packed[0] + packed[1]) + (packed[2] + packed[3])
        around_ref[f] = around
        send_ref[f, rows:] = around
        bottom = cells_ref[f, :, 0, :]
        top = cells_ref[f, :, depth - 1, :]
        bottom_ref[f] = bottom
        top_ref[f] = top
        axial_ref[f] = jnp.where(even, top, bottom)
        send_ref[f, :rows] = jnp.where(even, bottom, top)


def interior_kernel(chunk, x_ref, out_ref):
    fields, rows, depth, lanes = x_ref.shape
    lane = lax.broadcasted_iota(jnp.int32, (depth, lanes), 1)
    level = lax.broadcasted_iota(jnp.int32, (depth, lanes), 0)
    not_last_lane = lane < lanes - 1
    not_last_level = level < depth - 1

    def along(q, prims, direction, axis, size, keep):
        parts, reach = flux(q, prims, direction)
        ahead = [roll(v, size - 1, axis) for v in q]
        parts_ahead = [ahead[direction]] + [roll(v, size - 1, axis) for v in parts[1:]]
        reach = jnp.maximum(reach, roll(reach, size - 1, axis))
        above = faces(parts, parts_ahead, q, ahead, reach)
        above = [jnp.where(keep, v, 0.0) for v in above]
        return [v - roll(v, 1, axis) for v in above]

    def row(r):
        q = [x_ref[f, r] for f in range(fields)]
        prims = primitives(q)
        axial = along(q, prims, 1, 0, depth, not_last_level)
        around = along(q, prims, 3, 1, lanes, not_last_lane)
        partial = [
            v - AXIAL_HALF * a - AROUND_HALF * c for v, a, c in zip(q, axial, around)
        ]
        parts, reach = flux(q, prims, 2)
        return q, parts, reach, partial

    def step(i, carry):
        q_below, parts_below, reach_below, partial_below = carry
        for j in range(chunk):
            r = i * chunk + j
            q, parts, reach, partial = row(r)
            between = faces(parts_below, parts, q_below, q, jnp.maximum(reach_below, reach))
            between = [RADIAL_HALF * v for v in between]
            for f in range(fields):
                out_ref[f, jnp.maximum(r - 1, 0)] = partial_below[f] - between[f]
            partial_below = [v + b for v, b in zip(partial, between)]
            q_below, parts_below, reach_below = q, parts, reach
        return q_below, parts_below, reach_below, partial_below

    q = [x_ref[f, 0] for f in range(fields)]
    parts, reach = flux(q, primitives(q), 2)
    q, parts, reach, partial = lax.fori_loop(0, rows // chunk, step, (q, parts, reach, q))
    for f in range(fields):
        out_ref[f, rows - 1] = partial[f] - (2.0 * RADIAL_HALF) * parts[f]


def boundary_kernel(
    blk,
    count,
    table_ref,
    part_ref,
    bottom_ref,
    top_ref,
    axial_ref,
    ghost_ref,
    own_ref,
    beside_ref,
    other_ref,
    stencil_ref,
    out_ref,
    low_ref,
    high_ref,
    cells_ref,
    sent,
):
    fields, rows, depth, lanes = part_ref.shape
    halves = depth // 8
    lane8 = lax.broadcasted_iota(jnp.int32, (8, lanes), 1)
    level = lax.broadcasted_iota(jnp.int32, (8, lanes), 0)
    here = blk()
    is_even = here % 2 == 0
    first_lane = jnp.where(is_even, 2 * (halves - 1), 1)
    stencil = jnp.broadcast_to(stencil_ref[...], (8, lanes))
    weights = jnp.zeros((8, lanes), jnp.float32)
    for j in range(table_ref.shape[0]):
        weights = jnp.where(stencil == j, table_ref[j], weights)
    for j in range(rows // 8):
        span = slice(8 * j, 8 * j + 8)
        chosen = lane8 == 2 * halves * (8 * j + level) + first_lane
        end_lane = lane8 == jnp.where(is_even, 0, lanes - 1)
        lower, upper = [], []
        for f in range(fields):
            plane = ghost_ref[rows * f + 8 * j : rows * f + 8 * j + 8]
            packed_row = ghost_ref[fields * rows + f : fields * rows + f + 1]
            edge = jnp.sum(jnp.where(chosen, packed_row, 0.0), axis=1, keepdims=True)
            moved = jnp.where(is_even, roll(plane, 1, 1), roll(plane, lanes - 1, 1))
            beside = jnp.where(end_lane, edge, moved)
            ghost = weights * plane + (1.0 - weights) * beside
            near = axial_ref[f, span]
            below = jnp.where(here == count // 2, ghost, near)
            above = jnp.where(here == count // 2 - 1, ghost, near)
            lower.append(jnp.where(here == 0, bottom_ref[f, span], below))
            upper.append(jnp.where(here == count - 1, top_ref[f, span], above))
        below = faces_of(lower, [bottom_ref[f, span] for f in range(fields)], 1)
        above = faces_of([top_ref[f, span] for f in range(fields)], upper, 1)
        for f in range(fields):
            low_ref[f, span] = AXIAL_HALF * below[f]
            high_ref[f, span] = -AXIAL_HALF * above[f]
    even = lane8 % 2 == 0
    own = [own_ref[f] for f in range(fields)]
    besides = [beside_ref[f, rows:] for f in range(fields)]
    others = [other_ref[f] for f in range(fields)]
    lefts, rights = [], []
    for f in range(fields):
        left = jnp.where(is_even, besides[f], others[f])
        right = jnp.where(is_even, others[f], besides[f])
        lefts.append(jnp.where(even, own[f], roll(left, 1, 1)))
        rights.append(jnp.where(even, roll(right, lanes - 1, 1), own[f]))
    sides = faces_of(lefts, rights, 3)
    sides = [jnp.where(even, -AROUND_HALF * v, AROUND_HALF * v) for v in sides]
    ends = (lane8 == 0) | (lane8 == lanes - 1)
    copies = [
        pltpu.make_async_copy(cells_ref.at[f], out_ref.at[f], sent.at[f]) for f in range(fields)
    ]
    for f in range(fields):
        for r in range(rows):
            for h in range(halves):
                k = r * halves + h
                span = slice(8 * h, 8 * h + 8)
                tile = part_ref[f, r, span, :]
                tile = tile + jnp.where(ends, roll(sides[f], lanes - 1 - 2 * k, 1), 0.0)
                if h == 0:
                    tile = tile + jnp.where(level == 0, low_ref[f, r : r + 1, :], 0.0)
                if h == halves - 1:
                    tile = tile + jnp.where(level == 7, high_ref[f, r : r + 1, :], 0.0)
                cells_ref[f, r, span, :] = tile
        copies[f].start()
    for copy in copies:
        copy.wait()


def struct(*shape):
    return jax.ShapeDtypeStruct(shape, jnp.float32)


def shards(state, partner, stencil, weight_table):
    blk_count = lax.axis_size("blk")
    cycle_size = lax.axis_size("pass")
    blk_index = lax.axis_index("blk")
    half = blk_count // 2
    fields, rows, depth, lanes = state.shape
    smem = pl.BlockSpec(memory_space=pltpu.SMEM)
    vmem = pl.BlockSpec(memory_space=pltpu.VMEM)
    anywhere = pl.BlockSpec(memory_space=pl.ANY)
    params = pltpu.CompilerParams(vmem_limit_bytes=VMEM_LIMIT)
    blk = functools.partial(lax.axis_index, "blk")

    send, around, bottom, top, to_axial = pl.pallas_call(
        functools.partial(pack_kernel, blk),
        out_shape=[struct(fields, n, lanes) for n in (rows + 8, 8, rows, rows, rows)],
        in_specs=[anywhere],
        out_specs=[vmem] * 5,
        scratch_shapes=[pltpu.VMEM(state.shape, jnp.float32), pltpu.SemaphoreType.DMA((fields,))],
        compiler_params=params,
        name="pack",
    )(state)

    def at(p, b):
        return (p % cycle_size) * blk_count + b

    axial_pairs = []
    for p in range(cycle_size):
        for b in range(0, blk_count, 2):
            axial_pairs += [(at(p, b), at(p, b + 1)), (at(p, b + 1), at(p, b))]

    def far_pairs(s):
        pairs = []
        for p in range(cycle_size):
            pairs += [(at(p + s, half), at(p, half - 1)), (at(p - s, half - 1), at(p, half))]
        return pairs

    def side_pairs(s):
        pairs = []
        for p in range(cycle_size):
            for b in range(blk_count):
                pairs.append((at(p, b), at(p + (s if b % 2 == 0 else -s), b)))
        return pairs

    from_beside = lax.ppermute(send, AXES, side_pairs(1))
    from_other = lax.ppermute(around, AXES, side_pairs(-1))
    from_axial = lax.ppermute(to_axial, AXES, axial_pairs)

    rotation = partner[0] % cycle_size
    odd = rotation % 2 == 1
    even = blk_index % 2 == 0
    plane = jnp.where(odd, from_beside[:, :rows], send[:, :rows])
    edge = jnp.where(odd, around, from_other)
    edge = jnp.where(even, edge[:, 0], edge[:, 7])
    payload = jnp.concatenate(
        [plane.reshape(fields * rows, lanes), jnp.pad(edge, ((0, 8 - fields), (0, 0)))]
    )

    def far(s, values, cells):
        moved = lax.ppermute(values, AXES, far_pairs(s))
        part = pl.pallas_call(
            functools.partial(interior_kernel, CHUNK),
            out_shape=struct(*cells.shape),
            in_specs=[vmem],
            out_specs=vmem,
            compiler_params=params,
            name="interior",
        )(cells)
        return moved, part

    ghost, part = lax.switch(
        (rotation + 1) // 2 % (cycle_size // 2),
        [lambda a, c, s=s: far(2 * s, a, c) for s in range(cycle_size // 2)],
        payload,
        state,
    )
    return pl.pallas_call(
        functools.partial(boundary_kernel, blk, blk_count),
        out_shape=struct(*state.shape),
        in_specs=[smem] + [vmem] * 9,
        out_specs=anywhere,
        scratch_shapes=[pltpu.VMEM((fields, rows, lanes), jnp.float32)] * 2
        + [pltpu.VMEM(state.shape, jnp.float32), pltpu.SemaphoreType.DMA((fields,))],
        compiler_params=params,
        name="boundary",
    )(weight_table, part, bottom, top, from_axial, ghost, around, from_beside, from_other, stencil[None])


def solution(mesh):
    placed = (P(None, None, "blk", "pass"), P(), P("pass"), P())
    return jax.shard_map(
        shards, mesh=mesh, in_specs=placed, out_specs=P(None, None, "blk", "pass"), check_vma=False
    )
```

```python
import functools

import jax
import jax.numpy as jnp
from jax import lax
from jax.experimental import pallas as pl
from jax.experimental.pallas import tpu as pltpu
from jax.sharding import PartitionSpec as P

AXIAL_HALF = 0.2
RADIAL_HALF = 0.15
AROUND_HALF = 0.15
AXES = ("pass", "blk")
VMEM_LIMIT = 16 << 20
CHUNK = 4


def roll(value, amount, axis):
    amount = amount % value.shape[axis]
    return value if amount == 0 else pltpu.roll(value, amount, axis)


def primitives(q):
    inverse = 1.0 / q[0]
    u = [q[d] * inverse for d in (1, 2, 3)]
    pressure = 0.4 * (q[4] - 0.5 * (q[1] * u[0] + q[2] * u[1] + q[3] * u[2]))
    sound = jnp.sqrt(1.4 * pressure * inverse)
    return u, pressure, sound, q[4] + pressure


def flux(q, prims, direction):
    u, pressure, sound, enthalpy = prims
    speed = u[direction - 1]
    parts = [q[direction]]
    for k in (1, 2, 3):
        part = q[k] * speed
        parts.append(part + pressure if k == direction else part)
    parts.append(enthalpy * speed)
    return parts, jnp.abs(speed) + sound


def faces(flux_left, flux_right, left, right, reach):
    return [
        (fl + fr) - reach * (r - l) for fl, fr, l, r in zip(flux_left, flux_right, left, right)
    ]


def faces_of(left, right, direction):
    flux_left, reach_left = flux(left, primitives(left), direction)
    flux_right, reach_right = flux(right, primitives(right), direction)
    return faces(flux_left, flux_right, left, right, jnp.maximum(reach_left, reach_right))


def pack_kernel(
    blk, x_ref, send_ref, around_ref, bottom_ref, top_ref, axial_ref, cells_ref, arrived
):
    fields, rows, depth, lanes = x_ref.shape
    copies = [
        pltpu.make_async_copy(x_ref.at[f], cells_ref.at[f], arrived.at[f]) for f in range(fields)
    ]
    for copy in copies:
        copy.start()
    even = blk() % 2 == 0
    lane = lax.broadcasted_iota(jnp.int32, (8, lanes), 1)
    pair = lane // 2
    halves = depth // 8
    for f in range(fields):
        copies[f].wait()
        packed = [jnp.zeros((8, lanes), jnp.float32) for _ in range(4)]
        for r in range(rows):
            for h in range(halves):
                k = r * halves + h
                tile = cells_ref[f, r, 8 * h : 8 * h + 8, :]
                packed[k % 4] = jnp.where(pair == k, roll(tile, 2 * k + 1, 1), packed[k % 4])
        around = (packed[0] + packed[1]) + (packed[2] + packed[3])
        around_ref[f] = around
        send_ref[f, rows:] = around
        bottom = cells_ref[f, :, 0, :]
        top = cells_ref[f, :, depth - 1, :]
        bottom_ref[f] = bottom
        top_ref[f] = top
        axial_ref[f] = jnp.where(even, top, bottom)
        send_ref[f, :rows] = jnp.where(even, bottom, top)


def interior_kernel(chunk, x_ref, out_ref):
    fields, rows, depth, lanes = x_ref.shape
    lane = lax.broadcasted_iota(jnp.int32, (depth, lanes), 1)
    level = lax.broadcasted_iota(jnp.int32, (depth, lanes), 0)
    not_last_lane = lane < lanes - 1
    not_last_level = level < depth - 1

    def along(q, prims, direction, axis, size, keep):
        parts, reach = flux(q, prims, direction)
        ahead = [roll(v, size - 1, axis) for v in q]
        parts_ahead = [ahead[direction]] + [roll(v, size - 1, axis) for v in parts[1:]]
        reach = jnp.maximum(reach, roll(reach, size - 1, axis))
        above = faces(parts, parts_ahead, q, ahead, reach)
        above = [jnp.where(keep, v, 0.0) for v in above]
        return [v - roll(v, 1, axis) for v in above]

    def row(r):
        q = [x_ref[f, r] for f in range(fields)]
        prims = primitives(q)
        axial = along(q, prims, 1, 0, depth, not_last_level)
        around = along(q, prims, 3, 1, lanes, not_last_lane)
        partial = [
            v - AXIAL_HALF * a - AROUND_HALF * c for v, a, c in zip(q, axial, around)
        ]
        parts, reach = flux(q, prims, 2)
        return q, parts, reach, partial

    def step(i, carry):
        q_below, parts_below, reach_below, partial_below = carry
        for j in range(chunk):
            r = i * chunk + j
            q, parts, reach, partial = row(r)
            between = faces(parts_below, parts, q_below, q, jnp.maximum(reach_below, reach))
            between = [RADIAL_HALF * v for v in between]
            for f in range(fields):
                out_ref[f, jnp.maximum(r - 1, 0)] = partial_below[f] - between[f]
            partial_below = [v + b for v, b in zip(partial, between)]
            q_below, parts_below, reach_below = q, parts, reach
        return q_below, parts_below, reach_below, partial_below

    q = [x_ref[f, 0] for f in range(fields)]
    parts, reach = flux(q, primitives(q), 2)
    q, parts, reach, partial = lax.fori_loop(0, rows // chunk, step, (q, parts, reach, q))
    for f in range(fields):
        out_ref[f, rows - 1] = partial[f] - (2.0 * RADIAL_HALF) * parts[f]


def boundary_kernel(
    blk,
    count,
    table_ref,
    part_ref,
    bottom_ref,
    top_ref,
    axial_ref,
    ghost_ref,
    own_ref,
    beside_ref,
    other_ref,
    stencil_ref,
    out_ref,
    low_ref,
    high_ref,
    cells_ref,
    sent,
):
    fields, rows, depth, lanes = part_ref.shape
    halves = depth // 8
    lane8 = lax.broadcasted_iota(jnp.int32, (8, lanes), 1)
    level = lax.broadcasted_iota(jnp.int32, (8, lanes), 0)
    here = blk()
    is_even = here % 2 == 0
    first_lane = jnp.where(is_even, 2 * (halves - 1), 1)
    stencil = jnp.broadcast_to(stencil_ref[...], (8, lanes))
    weights = jnp.zeros((8, lanes), jnp.float32)
    for j in range(table_ref.shape[0]):
        weights = jnp.where(stencil == j, table_ref[j], weights)
    for j in range(rows // 8):
        span = slice(8 * j, 8 * j + 8)
        chosen = lane8 == 2 * halves * (8 * j + level) + first_lane
        end_lane = lane8 == jnp.where(is_even, 0, lanes - 1)
        lower, upper = [], []
        for f in range(fields):
            plane = ghost_ref[rows * f + 8 * j : rows * f + 8 * j + 8]
            packed_row = ghost_ref[fields * rows + f : fields * rows + f + 1]
            edge = jnp.sum(jnp.where(chosen, packed_row, 0.0), axis=1, keepdims=True)
            moved = jnp.where(is_even, roll(plane, 1, 1), roll(plane, lanes - 1, 1))
            beside = jnp.where(end_lane, edge, moved)
            ghost = weights * plane + (1.0 - weights) * beside
            near = axial_ref[f, span]
            below = jnp.where(here == count // 2, ghost, near)
            above = jnp.where(here == count // 2 - 1, ghost, near)
            lower.append(jnp.where(here == 0, bottom_ref[f, span], below))
            upper.append(jnp.where(here == count - 1, top_ref[f, span], above))
        below = faces_of(lower, [bottom_ref[f, span] for f in range(fields)], 1)
        above = faces_of([top_ref[f, span] for f in range(fields)], upper, 1)
        for f in range(fields):
            low_ref[f, span] = AXIAL_HALF * below[f]
            high_ref[f, span] = -AXIAL_HALF * above[f]
    even = lane8 % 2 == 0
    own = [own_ref[f] for f in range(fields)]
    besides = [beside_ref[f] for f in range(fields)]
    others = [other_ref[f] for f in range(fields)]
    lefts, rights = [], []
    for f in range(fields):
        left = jnp.where(is_even, besides[f], others[f])
        right = jnp.where(is_even, others[f], besides[f])
        lefts.append(jnp.where(even, own[f], roll(left, 1, 1)))
        rights.append(jnp.where(even, roll(right, lanes - 1, 1), own[f]))
    sides = faces_of(lefts, rights, 3)
    sides = [jnp.where(even, -AROUND_HALF * v, AROUND_HALF * v) for v in sides]
    ends = (lane8 == 0) | (lane8 == lanes - 1)
    copies = [
        pltpu.make_async_copy(cells_ref.at[f], out_ref.at[f], sent.at[f]) for f in range(fields)
    ]
    for f in range(fields):
        for r in range(rows):
            for h in range(halves):
                k = r * halves + h
                span = slice(8 * h, 8 * h + 8)
                tile = part_ref[f, r, span, :]
                tile = tile + jnp.where(ends, roll(sides[f], lanes - 1 - 2 * k, 1), 0.0)
                if h == 0:
                    tile = tile + jnp.where(level == 0, low_ref[f, r : r + 1, :], 0.0)
                if h == halves - 1:
                    tile = tile + jnp.where(level == 7, high_ref[f, r : r + 1, :], 0.0)
                cells_ref[f, r, span, :] = tile
        copies[f].start()
    for copy in copies:
        copy.wait()


def struct(*shape):
    return jax.ShapeDtypeStruct(shape, jnp.float32)


def shards(state, partner, stencil, weight_table):
    blk_count = lax.axis_size("blk")
    cycle_size = lax.axis_size("pass")
    blk_index = lax.axis_index("blk")
    half = blk_count // 2
    fields, rows, depth, lanes = state.shape
    smem = pl.BlockSpec(memory_space=pltpu.SMEM)
    vmem = pl.BlockSpec(memory_space=pltpu.VMEM)
    anywhere = pl.BlockSpec(memory_space=pl.ANY)
    params = pltpu.CompilerParams(vmem_limit_bytes=VMEM_LIMIT)
    blk = functools.partial(lax.axis_index, "blk")

    send, around, bottom, top, to_axial = pl.pallas_call(
        functools.partial(pack_kernel, blk),
        out_shape=[struct(fields, n, lanes) for n in (rows + 8, 8, rows, rows, rows)],
        in_specs=[anywhere],
        out_specs=[vmem] * 5,
        scratch_shapes=[pltpu.VMEM(state.shape, jnp.float32), pltpu.SemaphoreType.DMA((fields,))],
        compiler_params=params,
        name="pack",
    )(state)

    def at(p, b):
        return (p % cycle_size) * blk_count + b

    axial_pairs = []
    for p in range(cycle_size):
        for b in range(0, blk_count, 2):
            axial_pairs += [(at(p, b), at(p, b + 1)), (at(p, b + 1), at(p, b))]

    def far_pairs(s):
        pairs = []
        for p in range(cycle_size):
            pairs += [(at(p + s, half), at(p, half - 1)), (at(p - s, half - 1), at(p, half))]
        return pairs

    def side_pairs(s):
        pairs = []
        for p in range(cycle_size):
            for b in range(blk_count):
                pairs.append((at(p, b), at(p + (s if b % 2 == 0 else -s), b)))
        return pairs

    rotation = partner[0] % cycle_size
    odd = rotation % 2 == 1

    def with_plane(values, tile):
        moved = lax.ppermute(values, AXES, side_pairs(1))
        return moved[:, :rows], moved[:, rows:]

    def without_plane(values, tile):
        return values[:, :rows], lax.ppermute(tile, AXES, side_pairs(1))

    from_other = lax.ppermute(around, AXES, side_pairs(-1))
    from_axial = lax.ppermute(to_axial, AXES, axial_pairs)

    even = blk_index % 2 == 0
    plane, from_beside = lax.cond(odd, with_plane, without_plane, send, around)
    edge = jnp.where(odd, around, from_other)
    edge = jnp.where(even, edge[:, 0], edge[:, 7])
    payload = jnp.concatenate(
        [plane.reshape(fields * rows, lanes), jnp.pad(edge, ((0, 8 - fields), (0, 0)))]
    )

    def far(s, values, cells):
        moved = lax.ppermute(values, AXES, far_pairs(s))
        part = pl.pallas_call(
            functools.partial(interior_kernel, CHUNK),
            out_shape=struct(*cells.shape),
            in_specs=[vmem],
            out_specs=vmem,
            compiler_params=params,
            name="interior",
        )(cells)
        return moved, part

    ghost, part = lax.switch(
        (rotation + 1) // 2 % (cycle_size // 2),
        [lambda a, c, s=s: far(2 * s, a, c) for s in range(cycle_size // 2)],
        payload,
        state,
    )
    return pl.pallas_call(
        functools.partial(boundary_kernel, blk, blk_count),
        out_shape=struct(*state.shape),
        in_specs=[smem] + [vmem] * 9,
        out_specs=anywhere,
        scratch_shapes=[pltpu.VMEM((fields, rows, lanes), jnp.float32)] * 2
        + [pltpu.VMEM(state.shape, jnp.float32), pltpu.SemaphoreType.DMA((fields,))],
        compiler_params=params,
        name="boundary",
    )(weight_table, part, bottom, top, from_axial, ghost, around, from_beside, from_other, stencil[None])


def solution(mesh):
    placed = (P(None, None, "blk", "pass"), P(), P("pass"), P())
    return jax.shard_map(
        shards, mesh=mesh, in_specs=placed, out_specs=P(None, None, "blk", "pass"), check_vma=False
    )
```

```python
import functools

import jax
import jax.numpy as jnp
from jax import lax
from jax.experimental import pallas as pl
from jax.experimental.pallas import tpu as pltpu
from jax.sharding import PartitionSpec as P

AXIAL_HALF = 0.2
RADIAL_HALF = 0.15
AROUND_HALF = 0.15
AXES = ("pass", "blk")
VMEM_LIMIT = 16 << 20
CHUNK = 4


def roll(value, amount, axis):
    amount = amount % value.shape[axis]
    return value if amount == 0 else pltpu.roll(value, amount, axis)


def primitives(q):
    inverse = 1.0 / q[0]
    u = [q[d] * inverse for d in (1, 2, 3)]
    pressure = 0.4 * (q[4] - 0.5 * (q[1] * u[0] + q[2] * u[1] + q[3] * u[2]))
    sound = jnp.sqrt(1.4 * pressure * inverse)
    return u, pressure, sound, q[4] + pressure


def flux(q, prims, direction):
    u, pressure, sound, enthalpy = prims
    speed = u[direction - 1]
    parts = [q[direction]]
    for k in (1, 2, 3):
        part = q[k] * speed
        parts.append(part + pressure if k == direction else part)
    parts.append(enthalpy * speed)
    return parts, jnp.abs(speed) + sound


def faces(flux_left, flux_right, left, right, reach):
    return [
        (fl + fr) - reach * (r - l) for fl, fr, l, r in zip(flux_left, flux_right, left, right)
    ]


def faces_of(left, right, direction):
    flux_left, reach_left = flux(left, primitives(left), direction)
    flux_right, reach_right = flux(right, primitives(right), direction)
    return faces(flux_left, flux_right, left, right, jnp.maximum(reach_left, reach_right))


def pack_kernel(
    blk, x_ref, send_ref, around_ref, bottom_ref, top_ref, axial_ref, cells_ref, arrived
):
    fields, rows, depth, lanes = x_ref.shape
    copies = [
        pltpu.make_async_copy(x_ref.at[f], cells_ref.at[f], arrived.at[f]) for f in range(fields)
    ]
    for copy in copies:
        copy.start()
    even = blk() % 2 == 0
    lane = lax.broadcasted_iota(jnp.int32, (8, lanes), 1)
    pair = lane // 2
    halves = depth // 8
    for f in range(fields):
        copies[f].wait()
        packed = [jnp.zeros((8, lanes), jnp.float32) for _ in range(4)]
        for r in range(rows):
            for h in range(halves):
                k = r * halves + h
                tile = cells_ref[f, r, 8 * h : 8 * h + 8, :]
                packed[k % 4] = jnp.where(pair == k, roll(tile, 2 * k + 1, 1), packed[k % 4])
        around = (packed[0] + packed[1]) + (packed[2] + packed[3])
        around_ref[f] = around
        send_ref[f, rows:] = around
        bottom = cells_ref[f, :, 0, :]
        top = cells_ref[f, :, depth - 1, :]
        bottom_ref[f] = bottom
        top_ref[f] = top
        axial_ref[f] = jnp.where(even, top, bottom)
        send_ref[f, :rows] = jnp.where(even, bottom, top)


def interior_kernel(chunk, x_ref, out_ref):
    fields, rows, depth, lanes = x_ref.shape
    lane = lax.broadcasted_iota(jnp.int32, (depth, lanes), 1)
    level = lax.broadcasted_iota(jnp.int32, (depth, lanes), 0)
    not_last_lane = lane < lanes - 1
    not_last_level = level < depth - 1

    def along(q, prims, direction, axis, size, keep):
        parts, reach = flux(q, prims, direction)
        ahead = [roll(v, size - 1, axis) for v in q]
        parts_ahead = [ahead[direction]] + [roll(v, size - 1, axis) for v in parts[1:]]
        reach = jnp.maximum(reach, roll(reach, size - 1, axis))
        above = faces(parts, parts_ahead, q, ahead, reach)
        above = [jnp.where(keep, v, 0.0) for v in above]
        return [v - roll(v, 1, axis) for v in above]

    def row(r):
        q = [x_ref[f, r] for f in range(fields)]
        prims = primitives(q)
        axial = along(q, prims, 1, 0, depth, not_last_level)
        around = along(q, prims, 3, 1, lanes, not_last_lane)
        partial = [
            v - AXIAL_HALF * a - AROUND_HALF * c for v, a, c in zip(q, axial, around)
        ]
        parts, reach = flux(q, prims, 2)
        return q, parts, reach, partial

    def step(i, carry):
        q_below, parts_below, reach_below, partial_below = carry
        for j in range(chunk):
            r = i * chunk + j
            q, parts, reach, partial = row(r)
            between = faces(parts_below, parts, q_below, q, jnp.maximum(reach_below, reach))
            between = [RADIAL_HALF * v for v in between]
            for f in range(fields):
                out_ref[f, jnp.maximum(r - 1, 0)] = partial_below[f] - between[f]
            partial_below = [v + b for v, b in zip(partial, between)]
            q_below, parts_below, reach_below = q, parts, reach
        return q_below, parts_below, reach_below, partial_below

    q = [x_ref[f, 0] for f in range(fields)]
    parts, reach = flux(q, primitives(q), 2)
    q, parts, reach, partial = lax.fori_loop(0, rows // chunk, step, (q, parts, reach, q))
    for f in range(fields):
        out_ref[f, rows - 1] = partial[f] - (2.0 * RADIAL_HALF) * parts[f]


def boundary_kernel(
    blk,
    count,
    table_ref,
    part_ref,
    bottom_ref,
    top_ref,
    axial_ref,
    ghost_ref,
    own_ref,
    beside_ref,
    other_ref,
    stencil_ref,
    out_ref,
    low_ref,
    high_ref,
    cells_ref,
    sent,
):
    fields, rows, depth, lanes = part_ref.shape
    halves = depth // 8
    lane8 = lax.broadcasted_iota(jnp.int32, (8, lanes), 1)
    level = lax.broadcasted_iota(jnp.int32, (8, lanes), 0)
    here = blk()
    is_even = here % 2 == 0
    first_lane = jnp.where(is_even, 2 * (halves - 1), 1)
    stencil = jnp.broadcast_to(stencil_ref[...], (8, lanes))
    weights = jnp.zeros((8, lanes), jnp.float32)
    for j in range(table_ref.shape[0]):
        weights = jnp.where(stencil == j, table_ref[j], weights)
    for j in range(rows // 8):
        span = slice(8 * j, 8 * j + 8)
        chosen = lane8 == 2 * halves * (8 * j + level) + first_lane
        end_lane = lane8 == jnp.where(is_even, 0, lanes - 1)
        lower, upper = [], []
        for f in range(fields):
            plane = ghost_ref[rows * f + 8 * j : rows * f + 8 * j + 8]
            packed_row = ghost_ref[fields * rows + f : fields * rows + f + 1]
            edge = jnp.sum(jnp.where(chosen, packed_row, 0.0), axis=1, keepdims=True)
            moved = jnp.where(is_even, roll(plane, 1, 1), roll(plane, lanes - 1, 1))
            beside = jnp.where(end_lane, edge, moved)
            ghost = weights * plane + (1.0 - weights) * beside
            near = axial_ref[f, span]
            below = jnp.where(here == count // 2, ghost, near)
            above = jnp.where(here == count // 2 - 1, ghost, near)
            lower.append(jnp.where(here == 0, bottom_ref[f, span], below))
            upper.append(jnp.where(here == count - 1, top_ref[f, span], above))
        below = faces_of(lower, [bottom_ref[f, span] for f in range(fields)], 1)
        above = faces_of([top_ref[f, span] for f in range(fields)], upper, 1)
        for f in range(fields):
            low_ref[f, span] = AXIAL_HALF * below[f]
            high_ref[f, span] = -AXIAL_HALF * above[f]
    even = lane8 % 2 == 0
    own = [own_ref[f] for f in range(fields)]
    besides = [beside_ref[f, rows:] for f in range(fields)]
    others = [other_ref[f] for f in range(fields)]
    lefts, rights = [], []
    for f in range(fields):
        left = jnp.where(is_even, besides[f], others[f])
        right = jnp.where(is_even, others[f], besides[f])
        lefts.append(jnp.where(even, own[f], roll(left, 1, 1)))
        rights.append(jnp.where(even, roll(right, lanes - 1, 1), own[f]))
    sides = faces_of(lefts, rights, 3)
    sides = [jnp.where(even, -AROUND_HALF * v, AROUND_HALF * v) for v in sides]
    ends = (lane8 == 0) | (lane8 == lanes - 1)
    copies = [
        pltpu.make_async_copy(cells_ref.at[f], out_ref.at[f], sent.at[f]) for f in range(fields)
    ]
    for f in range(fields):
        for r in range(rows):
            for h in range(halves):
                k = r * halves + h
                span = slice(8 * h, 8 * h + 8)
                tile = part_ref[f, r, span, :]
                tile = tile + jnp.where(ends, roll(sides[f], lanes - 1 - 2 * k, 1), 0.0)
                if h == 0:
                    tile = tile + jnp.where(level == 0, low_ref[f, r : r + 1, :], 0.0)
                if h == halves - 1:
                    tile = tile + jnp.where(level == 7, high_ref[f, r : r + 1, :], 0.0)
                cells_ref[f, r, span, :] = tile
        copies[f].start()
    for copy in copies:
        copy.wait()


def struct(*shape):
    return jax.ShapeDtypeStruct(shape, jnp.float32)


def shards(state, partner, stencil, weight_table):
    blk_count = lax.axis_size("blk")
    cycle_size = lax.axis_size("pass")
    blk_index = lax.axis_index("blk")
    half = blk_count // 2
    fields, rows, depth, lanes = state.shape
    smem = pl.BlockSpec(memory_space=pltpu.SMEM)
    vmem = pl.BlockSpec(memory_space=pltpu.VMEM)
    anywhere = pl.BlockSpec(memory_space=pl.ANY)
    params = pltpu.CompilerParams(vmem_limit_bytes=VMEM_LIMIT)
    blk = functools.partial(lax.axis_index, "blk")

    send, around, bottom, top, to_axial = pl.pallas_call(
        functools.partial(pack_kernel, blk),
        out_shape=[struct(fields, n, lanes) for n in (rows + 8, 8, rows, rows, rows)],
        in_specs=[anywhere],
        out_specs=[vmem] * 5,
        scratch_shapes=[pltpu.VMEM(state.shape, jnp.float32), pltpu.SemaphoreType.DMA((fields,))],
        compiler_params=params,
        name="pack",
    )(state)

    def at(p, b):
        return (p % cycle_size) * blk_count + b

    axial_pairs = []
    for p in range(cycle_size):
        for b in range(0, blk_count, 2):
            axial_pairs += [(at(p, b), at(p, b + 1)), (at(p, b + 1), at(p, b))]

    def far_pairs(s):
        pairs = []
        for p in range(cycle_size):
            pairs += [(at(p + s, half), at(p, half - 1)), (at(p - s, half - 1), at(p, half))]
        return pairs

    def side_pairs(s):
        pairs = []
        for p in range(cycle_size):
            for b in range(blk_count):
                pairs.append((at(p, b), at(p + (s if b % 2 == 0 else -s), b)))
        return pairs

    from_beside = lax.ppermute(send, AXES, side_pairs(1))
    from_other = lax.ppermute(around, AXES, side_pairs(-1))
    from_axial = lax.ppermute(to_axial, AXES, axial_pairs)

    rotation = partner[0] % cycle_size
    odd = rotation % 2 == 1
    even = blk_index % 2 == 0
    plane = jnp.where(odd, from_beside[:, :rows], send[:, :rows])
    edge = jnp.where(odd, around, from_other)
    edge = jnp.where(even, edge[:, 0], edge[:, 7])
    payload = jnp.concatenate(
        [plane.reshape(fields * rows, lanes), jnp.pad(edge, ((0, 8 - fields), (0, 0)))]
    )

    part = pl.pallas_call(
        functools.partial(interior_kernel, CHUNK),
        out_shape=struct(*state.shape),
        in_specs=[vmem],
        out_specs=vmem,
        compiler_params=params,
        name="interior",
    )(state)
    ghost = lax.switch(
        (rotation + 1) // 2 % (cycle_size // 2),
        [
            lambda values, s=s: lax.ppermute(values, AXES, far_pairs(2 * s))
            for s in range(cycle_size // 2)
        ],
        payload,
    )
    return pl.pallas_call(
        functools.partial(boundary_kernel, blk, blk_count),
        out_shape=struct(*state.shape),
        in_specs=[smem] + [vmem] * 9,
        out_specs=anywhere,
        scratch_shapes=[pltpu.VMEM((fields, rows, lanes), jnp.float32)] * 2
        + [pltpu.VMEM(state.shape, jnp.float32), pltpu.SemaphoreType.DMA((fields,))],
        compiler_params=params,
        name="boundary",
    )(weight_table, part, bottom, top, from_axial, ghost, around, from_beside, from_other, stencil[None])


def solution(mesh):
    placed = (P(None, None, "blk", "pass"), P(), P("pass"), P())
    return jax.shard_map(
        shards, mesh=mesh, in_specs=placed, out_specs=P(None, None, "blk", "pass"), check_vma=False
    )
```
